32 devices in a mesh: tower: 4 (over y, x), rank: 8 (over z, core).
Axes of the slice: x: 2, y: 2, z: 4, core: 2. Of those that a mesh axis runs over, the one named last changes fastest.
Arguments:
- pooled: bfloat16 [2, 2048, 1024], P(None, ('tower', 'rank')), may hold values from -8 to 8
- feature_order: int32 [4, 4], P('tower'), may hold values from 0 to 3, as said below
- cross_weight: bfloat16 [4, 3, 512, 512], P('tower'), may hold values from -0.25 to 0.25
- cross_bias: float32 [4, 3, 512], P('tower'), may hold values from -3 to 3
- compress_weight: bfloat16 [4, 128, 512], P('tower'), may hold values from -0.25 to 0.25
- norm_gain: float32 [4, 128], P('tower'), may hold values from 0.1 to 1.9
- mlp_weight: bfloat16 [4096, 512], P(('tower', 'rank')), may hold values from -0.25 to 0.25
- mlp_bias: bfloat16 [4096], P(('tower', 'rank')), may hold values from -3 to 3
- out_weight: bfloat16 [4096], P(('tower', 'rank')), may hold values from -0.09375 to 0.09375
Outputs:
- logits: float32 [2, 8, 128], P(None, 'rank', 'tower')
The draws below stay inside these ranges and needn't reach their ends.
Inputs may be any that keep to these rules, and one draw needn't show every extreme that they name: `feature_order`: each row is an ordering of 0 to 3.
All inputs are finite; a program needn't handle non-finite values.
Results may differ from the reference program's by a relative error of at most 0.0076.
Values may be sent and summed in bfloat16 or wider, within the bound.
A program may use at most 64 MiB of HBM per device.

```python
import math
import jax
import jax.numpy as jnp
from jax import lax

E = 128
FT = 4
CD = 128
HID = 4096
LAYERS = 3
MB = 2
SAMP_DEV = 32
TD = 512
F = 16
ID = 512
SAMPLES = 1024
N_TOWER = 4
N_RANK = 8


def draw_pooled(key, part):
    first_key, second_key = jax.random.split(jax.random.fold_in(key, 11))
    shape = (MB, F * E, SAMPLES)
    base = jnp.clip(jax.random.normal(first_key, shape, jnp.float32), -4.0, 4.0)
    scales = jnp.exp(jax.random.uniform(second_key, (MB, 1, SAMPLES), jnp.float32, math.log(0.5), math.log(2.0)))
    return (base * scales).astype(jnp.bfloat16)


def draw_feature_order(key, part):
    keys = jax.random.split(jax.random.fold_in(key, 23), N_TOWER)
    return jax.vmap(lambda single: jax.random.permutation(single, FT))(keys).astype(jnp.int32)


def block_levels(key, shape, cuts, smallest, largest):
    loudness = 1.0
    for dim, blocks in cuts:
        steps = jax.random.uniform(jax.random.fold_in(jax.random.fold_in(key, 6), dim), (blocks,), jnp.float32, smallest / len(cuts), largest / len(cuts))
        loudness = loudness * jnp.repeat(jnp.exp(steps), shape[dim] // blocks).reshape((-1,) + (1,) * (len(shape) - 1 - dim))
    return loudness


def scatter_about(own_key, shape, width, bound, cuts=(), dtype=jnp.bfloat16):
    entries = width * jax.random.normal(own_key, shape, jnp.float32)
    if cuts:
        entries = entries * block_levels(own_key, shape, cuts, -0.22, 0.18)
    return jnp.clip(entries, -bound, bound).astype(dtype)


def setup_inputs(seed: int = 0) -> dict:
    key_list = jax.random.split(jax.random.key(seed), 10)
    return {
        "pooled": draw_pooled(jax.random.fold_in(key_list[9], 71), 0),
        "feature_order": draw_feature_order(jax.random.fold_in(key_list[9], 71), 0),
        "cross_weight": scatter_about(key_list[2], (N_TOWER, LAYERS, TD, TD), TD ** -0.5, 0.25, ((0, 4),)),
        "cross_bias": scatter_about(key_list[3], (N_TOWER, LAYERS, TD), 0.5, 3.0, ((0, 4),), jnp.float32),
        "compress_weight": scatter_about(key_list[4], (N_TOWER, CD, TD), TD ** -0.5, 0.25, ((0, 4),)),
        "norm_gain": jnp.clip(1.0 + 0.18 * jax.random.normal(key_list[5], (N_TOWER, CD), jnp.float32), 0.1, 1.9),
        "mlp_weight": scatter_about(key_list[6], (HID, ID), ID ** -0.5, 0.25, ((0, 32),)),
        "mlp_bias": scatter_about(key_list[7], (HID,), 0.5, 3.0, ((0, 32),)),
        "out_weight": scatter_about(key_list[8], (HID,), HID ** -0.5, 0.09375, ((0, 32),)),
    }


epsilon = 1e-06

def tower_block(first, weights, biases, compress, gain):
    first_f = first.astype(jnp.float32)
    current = first
    for layer in range(LAYERS):
        product = jnp.dot(weights[layer], current, preferred_element_type=jnp.float32) + biases[layer][:, None]
        current = (first_f * product + current.astype(jnp.float32)).astype(jnp.bfloat16)
    squeezed = jnp.dot(compress, current, preferred_element_type=jnp.float32)
    inverse_rms = lax.rsqrt(lax.optimization_barrier(jnp.mean(squeezed * squeezed, axis=0, keepdims=True)) + epsilon)
    return (squeezed * inverse_rms * gain[:, None]).astype(jnp.bfloat16)

def interact(joined):
    samples_now = joined.shape[1]
    values_f = joined.astype(jnp.float32).reshape(-1, CD, samples_now)
    gram = jnp.einsum('tck,uck->tuk', values_f, values_f, precision=lax.Precision.HIGHEST) / CD
    mixed = values_f + jnp.einsum('tuk,uck->tck', gram, values_f, precision=lax.Precision.HIGHEST)
    return mixed.reshape(-1, samples_now).astype(jnp.bfloat16)

def reference(pooled, feature_order, cross_weight, cross_bias, compress_weight, norm_gain, mlp_weight, mlp_bias, out_weight):
    results = []
    block_size = SAMP_DEV * N_TOWER
    for batch in range(MB):
        arrived = pooled[batch].reshape(N_TOWER, FT, E, SAMPLES)

        def one_tower(packed):
            blocks, slots, weights, biases, compress, gain = packed
            first = jnp.take(blocks, slots, axis=0).reshape(TD, SAMPLES)
            return tower_block(first, weights, biases, compress, gain)
        outputs = lax.map(one_tower, (arrived, feature_order, cross_weight, cross_bias, compress_weight, norm_gain))
        mixed = interact(outputs.reshape(ID, SAMPLES))
        pieces = mixed.reshape(ID, N_RANK, block_size).transpose(1, 0, 2)

        def one_block(piece):
            hidden = jnp.dot(mlp_weight, piece, preferred_element_type=jnp.float32) + mlp_bias.astype(jnp.float32)[:, None]
            return lax.optimization_barrier(jnp.sum(jax.nn.relu(hidden) * out_weight.astype(jnp.float32)[:, None], axis=0))
        results.append(lax.map(one_block, pieces))
    return jnp.stack(results)
```

```python
import functools

import jax
import jax.numpy as jnp
from jax import lax
from jax.experimental import pallas as pl
from jax.experimental.pallas import tpu as pltpu
from jax.sharding import PartitionSpec as P

E = 128
CD = 128
CORES = 2

epsilon = 1e-06
MESH = pl.DeviceIdType.MESH


def parent(source, target, chips):
    if target == 0 and source > 1:
        return 1
    if target == chips - 1 and source < chips - 2:
        return chips - 2
    return source


def fused(
    n_tower,
    n_rank,
    order,
    pooled,
    cross_w,
    cross_b,
    compress,
    gain,
    mlp_w,
    small,
    out,
    arrived,
    weights,
    compress_v,
    bias_v,
    gain_v,
    bias_c,
    gain_c,
    first,
    state_a,
    state_b,
    towers,
    mixed,
    rows,
    packs,
    hid_c,
    parts,
    load_sem,
    a2a_send,
    a2a_recv,
    row_send,
    row_recv,
    mate_send,
    mate_recv,
    pack_send,
    pack_recv,
    tower_send,
    tower_recv,
    part_send,
    part_recv,
):
    micro = pooled.shape[0]
    block = arrived.shape[-1]
    layers, td = cross_w.shape[1], cross_w.shape[2]
    chips = n_rank // CORES
    t = lax.axis_index("tower")
    r = lax.axis_index("rank")
    z = r // CORES
    c = lax.rem(r, CORES)
    mate = z * CORES + (1 - c)

    loads = [
        pltpu.make_async_copy(
            pooled.at[:, :, pl.ds(pl.multiple_of(r * block, block), block)], arrived.at[r], load_sem.at[0]
        ),
        pltpu.make_async_copy(cross_b.at[0], bias_v.at[pl.ds(0, layers)], load_sem.at[1]),
        pltpu.make_async_copy(gain, gain_v.at[pl.ds(0, 1)], load_sem.at[2]),
        pltpu.make_async_copy(small, packs.at[r], load_sem.at[3]),
        pltpu.make_async_copy(compress.at[0], compress_v, load_sem.at[4]),
        pltpu.make_async_copy(mlp_w, rows.at[r], load_sem.at[5]),
    ]
    w_loads = [pltpu.make_async_copy(cross_w.at[0, l], weights.at[l], load_sem.at[6 + l]) for l in range(layers)]

    barrier = pltpu.get_barrier_semaphore()
    for d in range(1, n_rank):
        pl.semaphore_signal(barrier, inc=1, device_id={"rank": lax.rem(r + d, n_rank)}, device_id_type=MESH)
    for d in range(1, n_tower):
        pl.semaphore_signal(barrier, inc=1, device_id={"tower": lax.rem(t + d, n_tower)}, device_id_type=MESH)
    for copy in loads + w_loads:
        copy.start()
    pl.semaphore_wait(barrier, n_rank + n_tower - 2)

    a2a = []
    for b in range(micro):
        for d in range(1, n_rank):
            peer = lax.rem(r + d, n_rank)
            copy = pltpu.make_async_remote_copy(
                src_ref=pooled.at[b, :, pl.ds(pl.multiple_of(peer * block, block), block)],
                dst_ref=arrived.at[r, b],
                send_sem=a2a_send.at[b, d - 1],
                recv_sem=a2a_recv.at[b, d - 1],
                device_id={"rank": peer},
                device_id_type=MESH,
            )
            copy.start()
            a2a.append(copy)

    def row_copy(source, target, src_ref):
        return pltpu.make_async_remote_copy(
            src_ref=src_ref,
            dst_ref=rows.at[source * CORES + c],
            send_sem=row_send.at[source, target],
            recv_sem=row_recv.at[source],
            device_id={"rank": target * CORES + c},
            device_id_type=MESH,
        )

    def mate_copy(source, src_ref):
        return pltpu.make_async_remote_copy(
            src_ref=src_ref,
            dst_ref=rows.at[source * CORES + c],
            send_sem=mate_send.at[source],
            recv_sem=mate_recv.at[source],
            device_id={"rank": mate},
            device_id_type=MESH,
        )

    packing = []
    for d in range(1, n_rank):
        copy = pltpu.make_async_remote_copy(
            src_ref=small,
            dst_ref=packs.at[r],
            send_sem=pack_send.at[d - 1],
            recv_sem=pack_recv.at[d - 1],
            device_id={"rank": lax.rem(r + d, n_rank)},
            device_id_type=MESH,
        )
        copy.start()
        packing.append(copy)

    for here in range(chips):

        @pl.when(z == here)
        def _():
            for target in sorted(range(chips), key=lambda q: abs(q - here)):
                if target != here and parent(here, target, chips) == here:
                    row_copy(here, target, mlp_w).start()
            mate_copy(here, mlp_w).start()

    def pass_on(near):
        for here in range(chips):

            @pl.when(z == here)
            def _():
                for source in sorted(range(chips), key=lambda q: abs(q - here)):
                    if source == here or (abs(source - here) == 1) != near:
                        continue
                    held = rows.at[source * CORES + c]
                    row_copy(source, here, held).wait_recv()
                    for target in range(chips):
                        if target not in (here, source) and parent(source, target, chips) == here:
                            row_copy(source, target, held).start()
                    mate_copy(source, held).start()

    for copy in loads:
        copy.wait()
    bias_c[...] = bias_v[...].T
    gain_c[...] = gain_v[...].T

    for copy in a2a:
        copy.wait_recv()
    per_feature = n_rank // order.shape[1]
    height = arrived.shape[2]
    for slot in range(order.shape[1]):
        feature = order[0, slot]
        for h in range(per_feature):
            for b in range(micro):
                first[
                    slot * E + h * height : slot * E + (h + 1) * height, b * block : (b + 1) * block
                ] = arrived[feature * per_feature + h, b]

    current, spare = first, state_a
    for l in range(layers):
        w_loads[l].wait()
        for m in range(0, td, E):
            here = slice(m, m + E)
            product = (
                jnp.dot(weights[l, here, :], current[...], preferred_element_type=jnp.float32)
                + bias_c[here, l : l + 1]
            )
            spare[here, :] = (
                first[here, :].astype(jnp.float32) * product + current[here, :].astype(jnp.float32)
            ).astype(jnp.bfloat16)
        current, spare = spare, (state_b if spare is state_a else state_a)
    squeezed = jnp.dot(compress_v[...], current[...], preferred_element_type=jnp.float32)
    inverse_rms = lax.rsqrt(jnp.mean(squeezed * squeezed, axis=0, keepdims=True) + epsilon)
    towers[t] = (squeezed * inverse_rms * gain_c[:, 0:1]).astype(jnp.bfloat16)

    exchange = []
    for d in range(1, n_tower):
        copy = pltpu.make_async_remote_copy(
            src_ref=towers.at[t],
            dst_ref=towers.at[t],
            send_sem=tower_send.at[d - 1],
            recv_sem=tower_recv.at[d - 1],
            device_id={"tower": lax.rem(t + d, n_tower)},
            device_id_type=MESH,
        )
        copy.start()
        exchange.append(copy)

    pass_on(True)
    for copy in packing:
        copy.wait_recv()
    turned_b = packs[:, 0, :].T
    turned_o = packs[:, 1, :].T
    for s in range(n_rank):
        hid_c[s, 0] = turned_b[:, s : s + 1]
        hid_c[s, 1] = turned_o[:, s : s + 1]

    for copy in exchange:
        copy.wait_recv()

    values = [towers[u].astype(jnp.float32) for u in range(n_tower)]
    gram = {}
    for u in range(n_tower):
        for v in range(u, n_tower):
            gram[u, v] = gram[v, u] = jnp.sum(values[u] * values[v], axis=0, keepdims=True) / CD
    for u in range(n_tower):
        total = values[u]
        for v in range(n_tower):
            total = total + gram[u, v] * values[v]
        mixed[u * CD : (u + 1) * CD, :] = total.astype(jnp.bfloat16)

    pass_on(False)
    side = 1 - 2 * (z // ((chips + 1) // 2))
    score = jnp.zeros((rows.shape[1], mixed.shape[1]), jnp.float32)
    for k in range(chips):
        source = lax.rem(z + side * k + chips, chips)
        for twin in range(CORES):
            s = source * CORES + (c if twin == 0 else 1 - c)
            if twin == 1:
                pltpu.make_async_remote_copy(
                    src_ref=rows.at[s],
                    dst_ref=rows.at[s],
                    send_sem=mate_send.at[source],
                    recv_sem=mate_recv.at[source],
                    device_id={"rank": mate},
                    device_id_type=MESH,
                ).wait_recv()
            hidden = jnp.dot(rows[s], mixed[...], preferred_element_type=jnp.float32) + hid_c[s, 0]
            score = score + jnp.maximum(hidden, 0.0) * hid_c[s, 1]
    parts[t] = jnp.sum(score, axis=0, keepdims=True)

    sums = []
    for d in range(1, n_tower):
        copy = pltpu.make_async_remote_copy(
            src_ref=parts.at[t],
            dst_ref=parts.at[t],
            send_sem=part_send.at[d - 1],
            recv_sem=part_recv.at[d - 1],
            device_id={"tower": lax.rem(t + d, n_tower)},
            device_id_type=MESH,
        )
        copy.start()
        sums.append(copy)

    for copy in a2a + packing + exchange:
        copy.wait_send()
    for here in range(chips):

        @pl.when(z == here)
        def _():
            for source in range(chips):
                for target in range(chips):
                    if target not in (here, source) and parent(source, target, chips) == here:
                        row_copy(source, target, rows.at[source * CORES + c]).wait_send()
                mate_copy(source, rows.at[source * CORES + c]).wait_send()

    for copy in sums:
        copy.wait_recv()
    logits = parts[0]
    for u in range(1, n_tower):
        logits = logits + parts[u]
    width = block // n_tower
    for u in range(n_tower):

        @pl.when(t == u)
        def _():
            for b in range(micro):
                out[b] = logits[:, b * block + u * width : b * block + (u + 1) * width]

    for copy in sums:
        copy.wait_send()


def in_one_kernel(
    n_tower, n_rank, pooled, order, cross_w, cross_b, compress, gain, mlp_w, mlp_bias, out_weight
):
    micro, height, samples = pooled.shape
    block = samples // n_rank
    _, layers, td, _ = cross_w.shape
    hid, width = mlp_w.shape
    chips = n_rank // CORES
    every = micro * block
    small = jnp.stack([mlp_bias, out_weight]).astype(jnp.float32)
    bf16, f32 = jnp.bfloat16, jnp.float32
    dma = pltpu.SemaphoreType.DMA
    hbm = pl.BlockSpec(memory_space=pl.ANY)
    return pl.pallas_call(
        functools.partial(fused, n_tower, n_rank),
        out_shape=jax.ShapeDtypeStruct((micro, 1, block // n_tower), f32),
        in_specs=[pl.BlockSpec(memory_space=pltpu.SMEM)] + [hbm] * 7,
        out_specs=pl.BlockSpec(memory_space=pltpu.VMEM),
        scratch_shapes=[
            pltpu.VMEM((n_rank, micro, height, block), bf16),
            pltpu.VMEM((layers, td, td), bf16),
            pltpu.VMEM((CD, td), bf16),
            pltpu.VMEM((8, td), f32),
            pltpu.VMEM((8, CD), f32),
            pltpu.VMEM((td, 8), f32),
            pltpu.VMEM((CD, 8), f32),
            pltpu.VMEM((td, every), bf16),
            pltpu.VMEM((td, every), bf16),
            pltpu.VMEM((td, every), bf16),
            pltpu.VMEM((n_tower, CD, every), bf16),
            pltpu.VMEM((width, every), bf16),
            pltpu.VMEM((n_rank, hid, width), bf16),
            pltpu.VMEM((n_rank, 2, hid), f32),
            pltpu.VMEM((n_rank, 2, hid, 1), f32),
            pltpu.VMEM((n_tower, 1, every), f32),
            dma((6 + layers,)),
            dma((micro, n_rank - 1)),
            dma((micro, n_rank - 1)),
            dma((chips, chips)),
            dma((chips,)),
            dma((chips,)),
            dma((chips,)),
            dma((n_rank - 1,)),
            dma((n_rank - 1,)),
            dma((n_tower - 1,)),
            dma((n_tower - 1,)),
            dma((n_tower - 1,)),
            dma((n_tower - 1,)),
        ],
        compiler_params=pltpu.CompilerParams(collective_id=0, has_side_effects=True),
    )(order, pooled, cross_w, cross_b, compress, gain, mlp_w, small)


def tower_block(first, weights, biases, compress, gain):
    first_f = first.astype(jnp.float32)
    current = first
    for layer in range(weights.shape[0]):
        product = (
            jnp.dot(weights[layer], current, preferred_element_type=jnp.float32)
            + biases[layer][:, None]
        )
        current = (first_f * product + current.astype(jnp.float32)).astype(jnp.bfloat16)
    squeezed = jnp.dot(compress, current, preferred_element_type=jnp.float32)
    inverse_rms = lax.rsqrt(jnp.mean(squeezed * squeezed, axis=0, keepdims=True) + epsilon)
    return (squeezed * inverse_rms * gain[:, None]).astype(jnp.bfloat16)


def interact(joined):
    samples_now = joined.shape[1]
    values_f = joined.astype(jnp.float32).reshape(-1, CD, samples_now)
    gram = jnp.einsum("tck,uck->tuk", values_f, values_f, precision=lax.Precision.HIGHEST) / CD
    mixed = values_f + jnp.einsum("tuk,uck->tck", gram, values_f, precision=lax.Precision.HIGHEST)
    return mixed.reshape(-1, samples_now).astype(jnp.bfloat16)


def logit_terms(hidden_rows, hidden_bias, hidden_out, features):
    hidden = (
        jnp.dot(hidden_rows, features, preferred_element_type=jnp.float32)
        + hidden_bias.astype(jnp.float32)[:, None]
    )
    return jnp.sum(
        jax.nn.relu(hidden) * hidden_out.astype(jnp.float32)[:, None], axis=0, keepdims=True
    )


def by_collectives(
    pooled,
    feature_order,
    cross_weight,
    cross_bias,
    compress_weight,
    norm_gain,
    mlp_weight,
    mlp_bias,
    out_weight,
):
    micro_count = pooled.shape[0]
    arriving = [
        lax.all_to_all(pooled[batch], "rank", split_axis=1, concat_axis=0, tiled=True)
        for batch in range(micro_count)
    ]
    hidden_rows, hidden_bias, hidden_out = (
        lax.all_gather(mlp_weight, "rank", axis=0, tiled=True),
        lax.all_gather(mlp_bias, "rank", axis=0, tiled=True),
        lax.all_gather(out_weight, "rank", axis=0, tiled=True),
    )
    results = []
    for batch in range(micro_count):
        arrived = arriving[batch]
        samples_here = arrived.shape[1]
        first = jnp.take(arrived.reshape(-1, E, samples_here), feature_order[0], axis=0).reshape(
            -1, samples_here
        )
        compressed = tower_block(
            first, cross_weight[0], cross_bias[0], compress_weight[0], norm_gain[0]
        )
        all_towers = lax.all_gather(compressed, "tower", axis=0, tiled=True)
        partial_value = logit_terms(hidden_rows, hidden_bias, hidden_out, interact(all_towers))
        logit_row = lax.psum_scatter(partial_value, "tower", scatter_dimension=1, tiled=True)
        results.append(logit_row)
    return jnp.stack(results)


def fits(mesh, pooled, mlp_w):
    height, hid = pooled.shape[1], mlp_w.shape[0]
    return mesh.shape["rank"] % CORES == 0 and E % height == 0 and height % 16 == 0 and hid % 128 == 0


def solution(mesh):
    def on_device(*args):
        if fits(mesh, args[0], args[6]):
            return in_one_kernel(mesh.shape["tower"], mesh.shape["rank"], *args)
        return by_collectives(*args)

    return jax.shard_map(
        on_device,
        mesh=mesh,
        in_specs=(
            P(None, ("tower", "rank"), None),
            P("tower", None),
            P("tower", None, None, None),
            P("tower", None, None),
            P("tower", None, None),
            P("tower", None),
            P(("tower", "rank"), None),
            P(("tower", "rank")),
            P(("tower", "rank")),
        ),
        out_specs=P(None, "rank", "tower"),
        check_vma=False,
    )
```

```python
import functools

import jax
import jax.numpy as jnp
from jax import lax
from jax.experimental import pallas as pl
from jax.experimental.pallas import tpu as pltpu
from jax.sharding import PartitionSpec as P

E = 128
CD = 128
CORES = 2

epsilon = 1e-06
MESH = pl.DeviceIdType.MESH


def fused(
    n_tower,
    n_rank,
    order,
    pooled,
    cross_w,
    cross_b,
    compress,
    gain,
    mlp_w,
    hid_b,
    hid_o,
    out,
    arrived,
    weights,
    compress_v,
    bias_v,
    flat_v,
    gain_v,
    bias_c,
    gain_c,
    first,
    state_a,
    state_b,
    towers,
    mixed,
    rows,
    packs_b,
    packs_o,
    flat_b,
    flat_o,
    hid_c,
    parts,
    load_sem,
    a2a_send,
    a2a_recv,
    row_send,
    row_recv,
    mate_send,
    mate_recv,
    pack_send,
    pack_recv,
    tower_send,
    tower_recv,
    part_send,
    part_recv,
):
    micro = pooled.shape[0]
    block = arrived.shape[-1]
    layers, td = cross_w.shape[1], cross_w.shape[2]
    smalls = ((hid_b, packs_b), (hid_o, packs_o))
    chips = n_rank // CORES
    t = lax.axis_index("tower")
    r = lax.axis_index("rank")
    z = r // CORES
    c = lax.rem(r, CORES)
    mate = z * CORES + (1 - c)

    loads = [
        pltpu.make_async_copy(
            pooled.at[:, :, pl.ds(pl.multiple_of(r * block, block), block)], arrived.at[r], load_sem.at[0]
        ),
        pltpu.make_async_copy(cross_b, bias_v, load_sem.at[1]),
        pltpu.make_async_copy(gain, gain_v, load_sem.at[2]),
        pltpu.make_async_copy(hid_b, packs_b.at[r], load_sem.at[3]),
        pltpu.make_async_copy(hid_o, packs_o.at[r], load_sem.at[4]),
        pltpu.make_async_copy(compress.at[0], compress_v, load_sem.at[5]),
        pltpu.make_async_copy(mlp_w, rows.at[r], load_sem.at[6]),
    ]
    w_loads = [pltpu.make_async_copy(cross_w.at[0, l], weights.at[l], load_sem.at[7 + l]) for l in range(layers)]

    barrier = pltpu.get_barrier_semaphore()
    for d in range(1, n_rank):
        pl.semaphore_signal(barrier, inc=1, device_id={"rank": lax.rem(r + d, n_rank)}, device_id_type=MESH)
    for d in range(1, n_tower):
        pl.semaphore_signal(barrier, inc=1, device_id={"tower": lax.rem(t + d, n_tower)}, device_id_type=MESH)
    for copy in loads + w_loads:
        copy.start()
    pl.semaphore_wait(barrier, n_rank + n_tower - 2)

    def spread(b, source, target, src_ref):
        return pltpu.make_async_remote_copy(
            src_ref=src_ref,
            dst_ref=arrived.at[source, b],
            send_sem=a2a_send.at[b, target],
            recv_sem=a2a_recv.at[b, source],
            device_id={"rank": target},
            device_id_type=MESH,
        )

    def chip_at(k):
        return lax.rem(z + k + chips, chips)

    others = [
        chip_at(k) * CORES + (c if twin == 0 else 1 - c)
        for k in sorted(range(chips), key=lambda k: -min(k, chips - k))
        for twin in range(CORES)
        if (k, twin) != (0, 0)
    ]
    a2a = []
    for b in range(micro):
        for peer in others:
            columns = pl.ds(pl.multiple_of(peer * block, block), block)
            copy = spread(b, r, peer, pooled.at[b, :, columns])
            copy.start()
            a2a.append(copy)

    half = rows.shape[1] // 2
    seen = set()

    def piece(k, h):
        return rows.at[chip_at(k) * CORES + c, pl.ds(h * half, half)]

    def row_copy(k, h, way, src_ref):
        return pltpu.make_async_remote_copy(
            src_ref=src_ref,
            dst_ref=piece(k, h),
            send_sem=row_send.at[abs(k), h, max(way, 0)],
            recv_sem=row_recv.at[chip_at(k), h],
            device_id={"rank": chip_at(way) * CORES + c},
            device_id_type=MESH,
        )

    def arrive(k, h):
        if k % chips and (k % chips, h) not in seen:
            seen.add((k % chips, h))
            row_copy(k, h, 1, piece(k, h)).wait_recv()

    row_sends = []

    def hop(s):
        for h, way in ((0, 1), (1, -1), (1, 1), (0, -1)):
            reach = chips // 2 if (h, way) in ((0, 1), (1, -1)) else (chips - 1) // 2
            if s < reach:
                k = -way * s
                if s:
                    arrive(k, h)
                copy = row_copy(k, h, way, piece(k, h) if s else mlp_w.at[pl.ds(h * half, half)])
                copy.start()
                row_sends.append(copy)

    def mate_copy(k, src_ref):
        return pltpu.make_async_remote_copy(
            src_ref=src_ref,
            dst_ref=rows.at[chip_at(k) * CORES + c],
            send_sem=mate_send.at[k],
            recv_sem=mate_recv.at[k],
            device_id={"rank": mate},
            device_id_type=MESH,
        )

    def share(k):
        for h in range(2):
            arrive(k, h)
        copy = mate_copy(k, rows.at[chip_at(k) * CORES + c] if k else mlp_w)
        copy.start()
        row_sends.append(copy)

    packing = []
    for d in range(1, n_rank):
        for i, (source, target) in enumerate(smalls):
            copy = pltpu.make_async_remote_copy(
                src_ref=source,
                dst_ref=target.at[r],
                send_sem=pack_send.at[i, d - 1],
                recv_sem=pack_recv.at[i, d - 1],
                device_id={"rank": lax.rem(r + d, n_rank)},
                device_id_type=MESH,
            )
            copy.start()
            packing.append(copy)

    hop(0)
    share(0)
    near = [k for k in range(1, chips) if min(k, chips - k) == 1]
    far = [k for k in sorted(range(1, chips), key=lambda k: min(k, chips - k)) if k not in near]

    for copy in loads:
        copy.wait()
    for l in range(layers):
        flat_v[l : l + 1, :] = bias_v[l]
    bias_c[...] = flat_v[...].T
    gain_c[...] = jnp.broadcast_to(gain_v[...], (8, CD)).T

    for b in range(micro):
        for peer in others:
            spread(b, peer, r, arrived.at[peer, b]).wait_recv()
    per_feature = n_rank // order.shape[1]
    height = arrived.shape[2]
    for slot in range(order.shape[1]):
        feature = order[0, slot]
        for h in range(per_feature):
            for b in range(micro):
                first[
                    slot * E + h * height : slot * E + (h + 1) * height, b * block : (b + 1) * block
                ] = arrived[feature * per_feature + h, b]

    current, spare = first, state_a
    for l in range(layers):
        w_loads[l].wait()
        for m in range(0, td, E):
            here = slice(m, m + E)
            product = (
                jnp.dot(weights[l, here, :], current[...], preferred_element_type=jnp.float32)
                + bias_c[here, l : l + 1]
            )
            spare[here, :] = (
                first[here, :].astype(jnp.float32) * product + current[here, :].astype(jnp.float32)
            ).astype(jnp.bfloat16)
        if l == layers - 1:
            hop(1)
        current, spare = spare, (state_b if spare is state_a else state_a)
    squeezed = jnp.dot(compress_v[...], current[...], preferred_element_type=jnp.float32)
    inverse_rms = lax.rsqrt(jnp.mean(squeezed * squeezed, axis=0, keepdims=True) + epsilon)
    towers[t] = (squeezed * inverse_rms * gain_c[:, 0:1]).astype(jnp.bfloat16)

    exchange = []
    for d in range(1, n_tower):
        copy = pltpu.make_async_remote_copy(
            src_ref=towers.at[t],
            dst_ref=towers.at[t],
            send_sem=tower_send.at[d - 1],
            recv_sem=tower_recv.at[d - 1],
            device_id={"tower": lax.rem(t + d, n_tower)},
            device_id_type=MESH,
        )
        copy.start()
        exchange.append(copy)

    for k in near:
        share(k)
    for step in range(2, chips // 2):
        hop(step)
    for copy in packing:
        copy.wait_recv()
    for s in range(n_rank):
        flat_b[s : s + 1, :] = packs_b[s].astype(jnp.float32)
        flat_o[s : s + 1, :] = packs_o[s].astype(jnp.float32)
    turned_b = flat_b[...].T
    turned_o = flat_o[...].T
    for s in range(n_rank):
        hid_c[s, 0] = turned_b[:, s : s + 1]
        hid_c[s, 1] = turned_o[:, s : s + 1]

    for copy in exchange:
        copy.wait_recv()

    values = [towers[u].astype(jnp.float32) for u in range(n_tower)]
    gram = {}
    for u in range(n_tower):
        for v in range(u, n_tower):
            gram[u, v] = gram[v, u] = jnp.sum(values[u] * values[v], axis=0, keepdims=True) / CD
    for u in range(n_tower):
        total = values[u]
        for v in range(n_tower):
            total = total + gram[u, v] * values[v]
        mixed[u * CD : (u + 1) * CD, :] = total.astype(jnp.bfloat16)

    score = jnp.zeros((rows.shape[1], mixed.shape[1]), jnp.float32)

    def add(s, score):
        hidden = jnp.dot(rows[s], mixed[...], preferred_element_type=jnp.float32) + hid_c[s, 0]
        return score + jnp.maximum(hidden, 0.0) * hid_c[s, 1]

    def add_mate(k, score):
        s = chip_at(k) * CORES + 1 - c
        pltpu.make_async_remote_copy(
            src_ref=rows.at[s],
            dst_ref=rows.at[s],
            send_sem=mate_send.at[k],
            recv_sem=mate_recv.at[k],
            device_id={"rank": mate},
            device_id_type=MESH,
        ).wait_recv()
        return add(s, score)

    for k in [0] + near:
        score = add(chip_at(k) * CORES + c, score)
    for k in [0] + near:
        score = add_mate(k, score)
    for k in far:
        share(k)
        score = add(chip_at(k) * CORES + c, score)
    for k in far:
        score = add_mate(k, score)
    parts[t] = jnp.sum(score, axis=0, keepdims=True)

    sums = []
    for d in range(1, n_tower):
        copy = pltpu.make_async_remote_copy(
            src_ref=parts.at[t],
            dst_ref=parts.at[t],
            send_sem=part_send.at[d - 1],
            recv_sem=part_recv.at[d - 1],
            device_id={"tower": lax.rem(t + d, n_tower)},
            device_id_type=MESH,
        )
        copy.start()
        sums.append(copy)

    for copy in a2a + packing + exchange + row_sends:
        copy.wait_send()
    for copy in sums:
        copy.wait_recv()
    logits = parts[0]
    for u in range(1, n_tower):
        logits = logits + parts[u]
    width = block // n_tower
    for u in range(n_tower):

        @pl.when(t == u)
        def _():
            for b in range(micro):
                out[b] = logits[:, b * block + u * width : b * block + (u + 1) * width]

    for copy in sums:
        copy.wait_send()


def in_one_kernel(
    n_tower, n_rank, pooled, order, cross_w, cross_b, compress, gain, mlp_w, mlp_bias, out_weight
):
    micro, height, samples = pooled.shape
    block = samples // n_rank
    _, layers, td, _ = cross_w.shape
    hid, width = mlp_w.shape
    chips = n_rank // CORES
    every = micro * block
    bf16, f32 = jnp.bfloat16, jnp.float32
    dma = pltpu.SemaphoreType.DMA
    hbm = pl.BlockSpec(memory_space=pl.ANY)
    return pl.pallas_call(
        functools.partial(fused, n_tower, n_rank),
        out_shape=jax.ShapeDtypeStruct((micro, 1, block // n_tower), f32),
        in_specs=[pl.BlockSpec(memory_space=pltpu.SMEM)] + [hbm] * 8,
        out_specs=pl.BlockSpec(memory_space=pltpu.VMEM),
        scratch_shapes=[
            pltpu.VMEM((n_rank, micro, height, block), bf16),
            pltpu.VMEM((layers, td, td), bf16),
            pltpu.VMEM((CD, td), bf16),
            pltpu.VMEM((layers, 1, td), f32),
            pltpu.VMEM((8, td), f32),
            pltpu.VMEM((1, CD), f32),
            pltpu.VMEM((td, 8), f32),
            pltpu.VMEM((CD, 8), f32),
            pltpu.VMEM((td, every), bf16),
            pltpu.VMEM((td, every), bf16),
            pltpu.VMEM((td, every), bf16),
            pltpu.VMEM((n_tower, CD, every), bf16),
            pltpu.VMEM((width, every), bf16),
            pltpu.VMEM((n_rank, hid, width), bf16),
            pltpu.VMEM((n_rank, 1, hid), bf16),
            pltpu.VMEM((n_rank, 1, hid), bf16),
            pltpu.VMEM((n_rank, hid), f32),
            pltpu.VMEM((n_rank, hid), f32),
            pltpu.VMEM((n_rank, 2, hid, 1), f32),
            pltpu.VMEM((n_tower, 1, every), f32),
            dma((7 + layers,)),
            dma((micro, n_rank)),
            dma((micro, n_rank)),
            dma((chips, 2, 2)),
            dma((chips, 2)),
            dma((chips,)),
            dma((chips,)),
            dma((2, n_rank - 1)),
            dma((2, n_rank - 1)),
            dma((n_tower - 1,)),
            dma((n_tower - 1,)),
            dma((n_tower - 1,)),
            dma((n_tower - 1,)),
        ],
        compiler_params=pltpu.CompilerParams(collective_id=0, has_side_effects=True),
    )(
        order,
        pooled,
        cross_w,
        cross_b.swapaxes(0, 1),
        compress,
        gain,
        mlp_w,
        mlp_bias[None],
        out_weight[None],
    )


def tower_block(first, weights, biases, compress, gain):
    first_f = first.astype(jnp.float32)
    current = first
    for layer in range(weights.shape[0]):
        product = (
            jnp.dot(weights[layer], current, preferred_element_type=jnp.float32)
            + biases[layer][:, None]
        )
        current = (first_f * product + current.astype(jnp.float32)).astype(jnp.bfloat16)
    squeezed = jnp.dot(compress, current, preferred_element_type=jnp.float32)
    inverse_rms = lax.rsqrt(jnp.mean(squeezed * squeezed, axis=0, keepdims=True) + epsilon)
    return (squeezed * inverse_rms * gain[:, None]).astype(jnp.bfloat16)


def interact(joined):
    samples_now = joined.shape[1]
    values_f = joined.astype(jnp.float32).reshape(-1, CD, samples_now)
    gram = jnp.einsum("tck,uck->tuk", values_f, values_f, precision=lax.Precision.HIGHEST) / CD
    mixed = values_f + jnp.einsum("tuk,uck->tck", gram, values_f, precision=lax.Precision.HIGHEST)
    return mixed.reshape(-1, samples_now).astype(jnp.bfloat16)


def logit_terms(hidden_rows, hidden_bias, hidden_out, features):
    hidden = (
        jnp.dot(hidden_rows, features, preferred_element_type=jnp.float32)
        + hidden_bias.astype(jnp.float32)[:, None]
    )
    return jnp.sum(
        jax.nn.relu(hidden) * hidden_out.astype(jnp.float32)[:, None], axis=0, keepdims=True
    )


def by_collectives(
    pooled,
    feature_order,
    cross_weight,
    cross_bias,
    compress_weight,
    norm_gain,
    mlp_weight,
    mlp_bias,
    out_weight,
):
    micro_count = pooled.shape[0]
    arriving = [
        lax.all_to_all(pooled[batch], "rank", split_axis=1, concat_axis=0, tiled=True)
        for batch in range(micro_count)
    ]
    hidden_rows, hidden_bias, hidden_out = (
        lax.all_gather(mlp_weight, "rank", axis=0, tiled=True),
        lax.all_gather(mlp_bias, "rank", axis=0, tiled=True),
        lax.all_gather(out_weight, "rank", axis=0, tiled=True),
    )
    results = []
    for batch in range(micro_count):
        arrived = arriving[batch]
        samples_here = arrived.shape[1]
        first = jnp.take(arrived.reshape(-1, E, samples_here), feature_order[0], axis=0).reshape(
            -1, samples_here
        )
        compressed = tower_block(
            first, cross_weight[0], cross_bias[0], compress_weight[0], norm_gain[0]
        )
        all_towers = lax.all_gather(compressed, "tower", axis=0, tiled=True)
        partial_value = logit_terms(hidden_rows, hidden_bias, hidden_out, interact(all_towers))
        logit_row = lax.psum_scatter(partial_value, "tower", scatter_dimension=1, tiled=True)
        results.append(logit_row)
    return jnp.stack(results)


def fits(mesh, pooled, mlp_w):
    height, hid = pooled.shape[1], mlp_w.shape[0]
    return mesh.shape["rank"] % CORES == 0 and E % height == 0 and height % 16 == 0 and hid % 128 == 0


def solution(mesh):
    def on_device(*args):
        if fits(mesh, args[0], args[6]):
            return in_one_kernel(mesh.shape["tower"], mesh.shape["rank"], *args)
        return by_collectives(*args)

    return jax.shard_map(
        on_device,
        mesh=mesh,
        in_specs=(
            P(None, ("tower", "rank"), None),
            P("tower", None),
            P("tower", None, None, None),
            P("tower", None, None),
            P("tower", None, None),
            P("tower", None),
            P(("tower", "rank"), None),
            P(("tower", "rank")),
            P(("tower", "rank")),
        ),
        out_specs=P(None, "rank", "tower"),
        check_vma=False,
    )
```
